128 devices in a mesh: dp: 4 (over y_hi, core), tensor: 32 (over x, y_lo, z).
Axes of the slice: x: 4, y: 4 (y_hi: 2, y_lo: 2; y = y_hi * 2 + y_lo), z: 4, core: 2. Of those that a mesh axis runs over, the one named last changes fastest.
Arguments:
- activations: bfloat16 [3072, 8192], P(('dp', 'tensor')), may hold values from -6 to 6
- cotangent: bfloat16 [3072, 8192], P(('dp', 'tensor')), may hold values from -6 to 6
- gate_pre: bfloat16 [3072, 28672], P('dp', 'tensor'), may hold values from -6 to 6
- up_pre: bfloat16 [3072, 28672], P('dp', 'tensor'), may hold values from -6 to 6
- down_weight: bfloat16 [28672, 8192], P('tensor'), may hold values from -0.03125 to 0.03125
- input_proj: bfloat16 [128, 8192], replicated, may hold values from -7 to 7
- output_proj: bfloat16 [64, 8192], replicated, may hold values from -7 to 7
- hidden_proj: bfloat16 [192, 28672], P(None, 'tensor'), may hold values from -7 to 7
- train_examples: int32 [4, 512], P('dp'), may hold values from 0 to 7, never falling along the last dimension, each value on 1 to 256 neighbouring positions
- val_examples: int32 [4, 256], P('dp'), may hold values from 0 to 1, never falling along the last dimension, each value on 1 to 192 neighbouring positions
Outputs:
- train_grads: float32 [32, 12288], P('dp', 'tensor')
- scores: float32 [32, 8], P('dp')
The draws below stay inside these ranges and needn't reach their ends.
Inputs may be any that keep to these rules, and one draw needn't show every extreme that they name: `train_examples`: example numbers do not fall along a group's tokens; each training example holds 1 to 256 tokens, one exactly 256. `val_examples`: example numbers do not fall along a group's tokens; each validation example holds 1 to 192 tokens.
All inputs are finite; a program needn't handle non-finite values.
Results may differ from the reference program's by a relative error of at most 0.0043.
Values may be sent and summed in bfloat16 or wider, within the bound.
No kernel may reach another device: no remote copies, remote signals or barrier semaphores. Data moves between devices by JAX's collectives and lax.ppermute only.
A program may use at most 128 MiB of HBM per device.

```python
import math
import jax
import jax.numpy as jnp
import numpy as np
from jax import lax

D = 8192
FF = 28672
RANK = 64
TRAIN_TOK = 512
VAL_TOK = 256
E_TRAIN = 8
E_VAL = 2
ROWS = 768
MOST_TRAIN = 256
MOST_VAL = 192
N_DP = 4


def projection_draw(key, salt, rows, cols, fan_in):
    base = jax.random.fold_in(key, salt)
    entry_key = jax.random.fold_in(base, 1)
    scale_key = jax.random.fold_in(base, 2)
    entries = jax.random.truncated_normal(entry_key, -5.0, 5.0, (rows, cols), jnp.float32)
    factor = jnp.exp(jax.random.uniform(scale_key, (rows, 1), jnp.float32, 0.0, math.log(10.0)))
    return (entries * factor / math.sqrt(fan_in)).astype(jnp.bfloat16)


def draw_input_proj(key, part):
    return projection_draw(key, 101, 2 * RANK, D, D)


def draw_output_proj(key, part):
    return projection_draw(key, 202, RANK, D, D)


def draw_hidden_proj(key, part):
    return projection_draw(key, 303, 3 * RANK, FF, FF)


def block_levels(own_key, extent, split, smallest, high):
    loudness = 1.0
    for axis_at, shards_of in split:
        heights = jax.random.uniform(jax.random.fold_in(jax.random.fold_in(own_key, 6), axis_at), (shards_of,), jnp.float32, smallest / len(split), high / len(split))
        loudness = loudness * jnp.repeat(jnp.exp(heights), extent[axis_at] // shards_of).reshape((-1,) + (1,) * (len(extent) - 1 - axis_at))
    return loudness


def length_profile(count, total, bound, lean):
    weights = [(1 << 20) // math.isqrt(rank ** lean) + 1 for rank in range(2, count + 1)]
    surplus, given = total - bound - (count - 1), [1] * (count - 1)
    while surplus > 0:
        free = [i for i in range(count - 1) if given[i] < bound]
        whole, left = sum([weights[i] for i in free]), surplus
        for i in free:
            more = min(bound - given[i], max(1, left * weights[i] // whole), surplus)
            given[i] = given[i] + more
            surplus = surplus - more
    return np.array([bound] + given)


def uneven_parts(rng, amount, total, bound, skew):
    if amount == 2:
        one = jax.random.randint(rng, (), max(1, total - bound), min(bound, total - 1) + 1)
        return jnp.stack([one, total - one])
    tallies = jnp.asarray(length_profile(amount, total, bound, skew), jnp.int32)
    couples = (amount - 1) // 2
    donor, taker = tallies[1:1 + 2 * couples:2], tallies[2:2 + 2 * couples:2]
    margin = jnp.minimum(donor - 1, bound - taker)
    passed = jax.random.randint(jax.random.fold_in(rng, 1), (couples,), 0, 1 << 20) % (margin + 1)
    tallies = tallies.at[1:1 + 2 * couples:2].set(donor - passed).at[2:2 + 2 * couples:2].set(taker + passed)
    return tallies[jax.random.permutation(jax.random.fold_in(rng, 2), amount)]


def bell_draw(rng, extent, spread, bound, cuts=(), kind=jnp.bfloat16):
    loudness = block_levels(rng, extent, cuts, -0.22, 0.18) if cuts else 1.0
    result = jax.random.normal(rng, extent, jnp.float32) * spread * loudness
    return jnp.minimum(jnp.maximum(result, -bound), bound).astype(kind)


def setup_inputs(seed: int = 0) -> dict:
    key_of = jax.random.split(jax.random.key(seed), 11)
    activations = bell_draw(key_of[0], (N_DP * ROWS, D), 1.0, 6.0, ((0, 128),))
    cotangent = bell_draw(key_of[1], (N_DP * ROWS, D), 1.0, 6.0, ((0, 128),))
    gate_pre = bell_draw(key_of[2], (N_DP * ROWS, FF), 1.0, 6.0, ((0, 4), (1, 32)))
    up_pre = bell_draw(key_of[3], (N_DP * ROWS, FF), 1.0, 6.0, ((0, 4), (1, 32)))
    down_weight = bell_draw(key_of[4], (FF, D), FF ** -0.5, 0.03125, ((0, 32),))
    input_proj = draw_input_proj(jax.random.fold_in(key_of[10], 71), 0)
    output_proj = draw_output_proj(jax.random.fold_in(key_of[10], 71), 0)
    hidden_proj = draw_hidden_proj(jax.random.fold_in(key_of[10], 71), 0)
    train_examples = jax.vmap(lambda own: jnp.searchsorted(jnp.cumsum(uneven_parts(own, E_TRAIN, TRAIN_TOK, MOST_TRAIN, 1)), jnp.arange(TRAIN_TOK), side="right"))(jax.random.split(key_of[8], N_DP)).reshape((N_DP, TRAIN_TOK)).astype(jnp.int32)
    val_examples = jax.vmap(lambda own: jnp.searchsorted(jnp.cumsum(uneven_parts(own, E_VAL, VAL_TOK, MOST_VAL, 1)), jnp.arange(VAL_TOK), side="right"))(jax.random.split(key_of[9], N_DP)).reshape((N_DP, VAL_TOK)).astype(jnp.int32)
    return dict(activations=activations, cotangent=cotangent, gate_pre=gate_pre, up_pre=up_pre, down_weight=down_weight, input_proj=input_proj, output_proj=output_proj, hidden_proj=hidden_proj, train_examples=train_examples, val_examples=val_examples)


def project_rows(rows, proj):
    return lax.dot_general(rows, proj, (((1,), (1,)), ((), ())), preferred_element_type=jnp.float32)

def hidden_terms(grad_rows, gate, up, down_weight, hidden_proj, rank):
    hidden_grad = lax.dot_general(grad_rows, down_weight, (((1,), (1,)), ((), ())), preferred_element_type=jnp.float32)
    gate = gate.astype(jnp.float32)
    up = up.astype(jnp.float32)
    sigmoid_gate = jax.nn.sigmoid(gate)
    activated = gate * sigmoid_gate
    gate_grad = (hidden_grad * up * sigmoid_gate * (1.0 + gate * (1.0 - sigmoid_gate))).astype(jnp.bfloat16)
    up_grad = (hidden_grad * activated).astype(jnp.bfloat16)
    hidden_act = (activated * up).astype(jnp.bfloat16)
    parts = [project_rows(value, hidden_proj[k * rank:(k + 1) * rank]) for k, value in enumerate((gate_grad, up_grad, hidden_act))]
    return jnp.concatenate(parts, axis=1)

def outer_sum(left, right, example_ids, count):
    number = left.shape[0]
    rank = left.shape[1]
    onehot = (example_ids[:, None] == jnp.arange(count, dtype=jnp.int32)[None, :]).astype(jnp.float32)
    weighted = (onehot[:, :, None] * left[:, None, :]).reshape(number, count * rank)
    block = lax.dot_general(weighted, right, (((0,), (0,)), ((), ())), precision=lax.Precision.HIGHEST, preferred_element_type=jnp.float32)
    return block.reshape(count, rank * right.shape[1])

def example_grads(hidden_side, input_side, output_side, example_ids, count, rank):
    gate_block = outer_sum(hidden_side[:, :rank], input_side[:, :rank], example_ids, count)
    up_block = outer_sum(hidden_side[:, rank:2 * rank], input_side[:, rank:], example_ids, count)
    down_block = outer_sum(output_side, hidden_side[:, 2 * rank:], example_ids, count)
    return jnp.concatenate([gate_block, up_block, down_block], axis=1)

def normalize_rows(grads):
    return grads / jnp.sqrt(lax.optimization_barrier(jnp.mean(grads * grads, axis=1, keepdims=True)) + 1e-06)

def reference(activations, cotangent, gate_pre, up_pre, down_weight, input_proj, output_proj, hidden_proj, train_examples, val_examples):
    train_units = []
    val_units = []
    for group in range(N_DP):
        low = group * ROWS
        grad_rows = cotangent[low:low + ROWS]
        hidden_side = hidden_terms(grad_rows, gate_pre[low:low + ROWS], up_pre[low:low + ROWS], down_weight, hidden_proj, RANK)
        output_side = project_rows(grad_rows, output_proj)
        input_side = project_rows(activations[low:low + ROWS], input_proj)
        train_grads = example_grads(hidden_side[:TRAIN_TOK], input_side[:TRAIN_TOK], output_side[:TRAIN_TOK], train_examples[group], E_TRAIN, RANK)
        val_grads = example_grads(hidden_side[TRAIN_TOK:], input_side[TRAIN_TOK:], output_side[TRAIN_TOK:], val_examples[group], E_VAL, RANK)
        train_units.append(normalize_rows(train_grads))
        val_units.append(normalize_rows(val_grads))
    train_all = jnp.concatenate(train_units, axis=0)
    val_all = jnp.concatenate(val_units, axis=0)
    scores = lax.dot_general(train_all, val_all, (((1,), (1,)), ((), ())), precision=lax.Precision.HIGHEST, preferred_element_type=jnp.float32)
    return (train_all, scores / math.sqrt(3 * RANK * RANK))
```

```python
import functools
import math

import jax
import jax.numpy as jnp
from jax import lax
from jax.experimental import pallas as pl
from jax.experimental.pallas import tpu as pltpu
from jax.sharding import PartitionSpec as P

E_TRAIN = 8
E_VAL = 2
E_ALL = E_TRAIN + E_VAL
NX, NY, NZ = 4, 2, 4


f32 = jnp.float32
bf16 = jnp.bfloat16


def shard_at(x, y, z):
    return (x % NX) * (NY * NZ) + (y % NY) * NZ + z % NZ


def shift(value, dx, dy, dz):
    pairs = [
        (shard_at(x, y, z), shard_at(x + dx, y + dy, z + dz))
        for x in range(NX)
        for y in range(NY)
        for z in range(NZ)
    ]
    return lax.ppermute(value, "tensor", pairs)


def dot_t(a, b, precision=None):
    return lax.dot_general(
        a, b, (((1,), (1,)), ((), ())), precision=precision, preferred_element_type=f32
    )


def side_kernel(n, ids_ref, hg_ref, gate_ref, up_ref, proj_ref, out_ref, gg_ref, ug_ref):
    rows = gate_ref.shape[1]
    rank = out_ref.shape[1] // 2
    for k in range(n):
        at = ids_ref[k]
        grad = hg_ref[pl.ds(k * rows, rows), :]
        gate = gate_ref[at].astype(f32)
        up = up_ref[at].astype(f32)
        sig = jax.nn.sigmoid(gate)
        gg = grad * up * sig * (1.0 + gate * (1.0 - sig))
        ug = grad * (gate * sig)
        gg_ref[pl.ds(k * rows, rows), :] = gg.astype(bf16).astype(f32)
        ug_ref[pl.ds(k * rows, rows), :] = ug.astype(bf16).astype(f32)
    out_ref[:, :rank] = dot_t(gg_ref[...].astype(bf16), proj_ref[0])
    out_ref[:, rank:] = dot_t(ug_ref[...].astype(bf16), proj_ref[1])


def side_chunk(ids, hidden_grad, gate3, up3, proj3):
    n = ids.shape[0]
    rows, width = hidden_grad.shape
    rank = proj3.shape[1]
    vm = pl.BlockSpec(memory_space=pltpu.VMEM)
    return pl.pallas_call(
        functools.partial(side_kernel, n),
        out_shape=jax.ShapeDtypeStruct((rows, 2 * rank), f32),
        in_specs=[pl.BlockSpec(memory_space=pltpu.SMEM), vm, vm, vm, vm],
        out_specs=vm,
        scratch_shapes=[pltpu.VMEM((rows, width), f32), pltpu.VMEM((rows, width), f32)],
        name="side_chunk",
    )(ids, hidden_grad, gate3, up3, proj3)


def place_kernel(counts, ids_ref, *refs):
    pieces, g3_ref, out_ref, all_ref = refs[:-3], refs[-3], refs[-2], refs[-1]
    rows = all_ref.shape[1]
    at = 0
    for piece, n in zip(pieces, counts):
        for k in range(n):
            all_ref[ids_ref[at]] = piece[pl.ds(k * rows, rows), :]
            at += 1
    whole = all_ref[...].reshape(all_ref.shape[0] * rows, all_ref.shape[2])
    half = all_ref.shape[2]
    out_ref[:half, :] = whole.T.astype(bf16)
    out_ref[half:, :] = g3_ref[...].astype(bf16)


def place(ids, pieces, g3):
    shards = ids.shape[0]
    counts = [p.shape[0] // (g3.shape[1] // shards) for p in pieces]
    rows = g3.shape[1] // shards
    cols = pieces[0].shape[1]
    vm = pl.BlockSpec(memory_space=pltpu.VMEM)
    return pl.pallas_call(
        functools.partial(place_kernel, counts),
        out_shape=jax.ShapeDtypeStruct((cols + g3.shape[0], g3.shape[1]), bf16),
        in_specs=[pl.BlockSpec(memory_space=pltpu.SMEM)] + [vm] * (len(pieces) + 1),
        out_specs=vm,
        scratch_shapes=[pltpu.VMEM((shards, rows, cols), f32)],
        name="place_sides",
    )(ids, *pieces, g3)


def per_device(
    activations,
    cotangent,
    gate_pre,
    up_pre,
    down_weight,
    input_proj,
    output_proj,
    hidden_proj,
    train_examples,
    val_examples,
):
    rank = output_proj.shape[0]
    per, width = cotangent.shape
    n_dev = NX * NY * NZ
    tokens = per * n_dev
    ff = gate_pre.shape[1]
    tiles = width // 128
    cut_a = (tiles * 28 // 64) * 128
    half_a = (cut_a // 256) * 128
    half_b = ((width - cut_a) // 256) * 128

    me = lax.axis_index("tensor")
    mx, my, mz = me // (NY * NZ), (me // NZ) % NY, me % NZ

    own = cotangent
    xm, xp = shift(own, 1, 0, 0), shift(own, -1, 0, 0)
    zm, zp = shift(own, 0, 0, 1), shift(own, 0, 0, -1)
    y0 = shift(own, 0, 1, 0)

    io = jnp.concatenate([dot_t(activations, input_proj), dot_t(own, output_proj)], axis=1)
    io = io.astype(bf16)
    io_all = lax.all_to_all(
        jnp.broadcast_to(io[None], (n_dev, *io.shape)), "tensor", 0, 0, tiled=True
    ).reshape(tokens, 3 * rank).astype(f32)
    input_side, output_side = io_all[:, : 2 * rank], io_all[:, 2 * rank :]

    ids = jnp.concatenate([train_examples[0], val_examples[0] + E_TRAIN])
    onehot = (ids[:, None] == jnp.arange(E_ALL, dtype=jnp.int32)[None, :]).astype(f32)

    gate_f, up_f = gate_pre.astype(f32), up_pre.astype(f32)
    act = (gate_f * jax.nn.sigmoid(gate_f) * up_f).astype(bf16)
    h3 = dot_t(act, hidden_proj[2 * rank :])
    h3_by_example = (onehot[:, :, None] * h3[:, None, :]).reshape(tokens, E_ALL * rank)
    g3 = lax.dot_general(
        output_side,
        h3_by_example,
        (((0,), (0,)), ((), ())),
        precision=lax.Precision.HIGHEST,
        preferred_element_type=f32,
    )
    g3 = jnp.pad(g3, ((0, 0), (0, tokens - E_ALL * rank)))

    def line(centre, m, p, axis):
        step = (1, 0, 0) if axis == 0 else (0, 0, 1)
        back = tuple(-s for s in step)
        two_a = shift(m[:, :cut_a], *step)
        two_b = shift(p[:, cut_a:], *back)
        return two_a, two_b

    def planes(m_x, p_x, x2a, m_z, p_z, z2b):
        xa = jnp.concatenate([m_x[:, :cut_a], p_x[:, :cut_a], x2a], axis=0)
        zb = jnp.concatenate([m_z[:, cut_a:], p_z[:, cut_a:], z2b], axis=0)
        am, ap = shift(xa, 0, 0, 1), shift(xa, 0, 0, -1)
        bm, bp = shift(zb, 1, 0, 0), shift(zb, -1, 0, 0)
        a2 = jnp.concatenate(
            [shift(am[:, :half_a], 0, 0, 1), shift(ap[:, half_a:], 0, 0, -1)], axis=1
        )
        b2 = jnp.concatenate(
            [shift(bm[:, :half_b], 1, 0, 0), shift(bp[:, half_b:], -1, 0, 0)], axis=1
        )
        return jnp.concatenate([am, ap, a2], axis=0), jnp.concatenate([bm, bp, b2], axis=0)

    x2a, x2b = line(own, xm, xp, 0)
    z2a, z2b = line(own, zm, zp, 2)
    x2, z2 = jnp.concatenate([x2a, x2b], axis=1), jnp.concatenate([z2a, z2b], axis=1)
    yxm, yxp, yx2 = shift(xm, 0, 1, 0), shift(xp, 0, 1, 0), shift(x2, 0, 1, 0)
    yzm, yzp = shift(y0, 0, 0, 1), shift(y0, 0, 0, -1)
    yz2a, yz2b = line(y0, yzm, yzp, 2)
    yz2 = jnp.concatenate([yz2a, yz2b], axis=1)

    pa, pb = planes(xm, xp, x2a, zm, zp, z2b)
    ypa, ypb = planes(yxm, yxp, yx2[:, :cut_a], yzm, yzp, yz2b)

    def plane_grad(a, b):
        by_a = dot_t(a, down_weight[:, :cut_a]).reshape(3, 3, per, ff)
        by_b = dot_t(b, down_weight[:, cut_a:]).reshape(3, 3, per, ff)
        return (jnp.swapaxes(by_b, 0, 1) + by_a).reshape(9 * per, ff)

    off3 = (-1, 1, 2)
    line_offs = [(0, 0)] + [(d, 0) for d in off3] + [(0, d) for d in off3]
    plane_offs = [(dx, dz) for dz in off3 for dx in off3]

    def ids_of(offs, dy):
        return jnp.stack([shard_at(mx + dx + NX, my + dy, mz + dz + NZ) for dx, dz in offs])

    gate3, up3 = gate_pre.reshape(n_dev, per, ff), up_pre.reshape(n_dev, per, ff)
    proj3 = hidden_proj[: 2 * rank].reshape(2, rank, ff)
    chunk_ids, sides = [], []
    for dy, rows in ((0, [own, xm, xp, x2, zm, zp, z2]), (1, [y0, yxm, yxp, yx2, yzm, yzp, yz2])):
        grad = dot_t(jnp.concatenate(rows, axis=0), down_weight)
        chunk_ids.append(ids_of(line_offs, dy))
        sides.append(side_chunk(chunk_ids[-1], grad, gate3, up3, proj3))
    for dy, (a, b) in ((0, (pa, pb)), (1, (ypa, ypb))):
        grad = plane_grad(a, b)
        chunk_ids.append(ids_of(plane_offs, dy))
        sides.append(side_chunk(chunk_ids[-1], grad, gate3, up3, proj3))

    rows_out = place(jnp.concatenate(chunk_ids).astype(jnp.int32), sides, g3)
    own_rows = 3 * rank // n_dev
    arrived = lax.all_to_all(
        rows_out.reshape(n_dev, own_rows, tokens), "tensor", 0, 0, tiled=True
    )
    summed = jnp.sum(arrived.astype(f32), axis=0)

    by_example = (onehot.T[:, None, :] * summed[None]).reshape(E_ALL * own_rows, tokens)
    both = lax.dot_general(
        by_example,
        input_side,
        (((1,), (0,)), ((), ())),
        precision=lax.Precision.HIGHEST,
        preferred_element_type=f32,
    ).reshape(E_ALL, own_rows, 2, rank)
    row = me * own_rows + jnp.arange(own_rows)
    block = (row // rank)[None, :, None]
    down = jnp.swapaxes(summed[:, : E_ALL * rank].reshape(own_rows, E_ALL, rank), 0, 1)
    raw = jnp.where(block == 0, both[:, :, 0], jnp.where(block == 1, both[:, :, 1], down))
    raw = raw.reshape(E_ALL, own_rows * rank)

    val_raw = lax.all_gather(raw[E_TRAIN:], "dp", axis=0, tiled=True)
    products = lax.dot_general(
        raw[:E_TRAIN],
        val_raw,
        (((1,), (1,)), ((), ())),
        precision=lax.Precision.HIGHEST,
        preferred_element_type=f32,
    )
    n_val = val_raw.shape[0]
    sums = jnp.concatenate(
        [
            products,
            jnp.sum(raw[:E_TRAIN] * raw[:E_TRAIN], axis=1)[:, None],
            jnp.sum(val_raw * val_raw, axis=1)[:, None],
        ],
        axis=1,
    )
    sums = lax.all_to_all(
        jnp.broadcast_to(sums[None], (n_dev, *sums.shape)), "tensor", 0, 0, tiled=True
    )
    sums = jnp.sum(sums, axis=0)
    full = 3 * rank * rank
    train_scale = jnp.sqrt(sums[:, n_val] / full + 1e-06)
    val_scale = jnp.sqrt(sums[:, n_val + 1] / full + 1e-06)
    train_units = raw[:E_TRAIN] / train_scale[:, None]
    scores = sums[:, :n_val] / (train_scale[:, None] * val_scale[None, :]) / math.sqrt(full)
    return (train_units, scores)


def solution(mesh):
    return jax.shard_map(
        per_device,
        mesh=mesh,
        in_specs=(
            P(("dp", "tensor"), None),
            P(("dp", "tensor"), None),
            P("dp", "tensor"),
            P("dp", "tensor"),
            P("tensor", None),
            P(),
            P(),
            P(None, "tensor"),
            P("dp", None),
            P("dp", None),
        ),
        out_specs=(P("dp", "tensor"), P("dp", None)),
        check_vma=False,
    )
```
